32 devices in a mesh: ctx: 8 (over z, y), head: 4 (over x, core).
Axes of the slice: x: 2, y: 2, z: 4, core: 2. Of those that a mesh axis runs over, the one named last changes fastest.
Arguments:
- queries: bfloat16 [16384, 3072], P('ctx', 'head'), may hold values from -11 to 11
- keys: bfloat16 [16384, 3072], P('ctx', 'head'), may hold values from -0.5 to 0.5
- values: bfloat16 [16384, 3072], P('ctx', 'head'), may hold values from -6 to 6
- documents: int32 [16384], P('ctx'), may hold values from 0 to 7, never falling along the last dimension, each value on 1 to 8192 neighbouring positions
- norm_gain: float32 [3072], P('head'), may hold values from 0.5 to 1.5
Outputs:
- normed: bfloat16 [16384, 3072], P('ctx', 'head')
The draws below stay inside these ranges and needn't reach their ends.
Inputs may be any that keep to these rules, and one draw needn't show every extreme that they name: `documents`: document numbers never fall along the window; each document has 1 to 8192 tokens.
All inputs are finite; a program needn't handle non-finite values.
Results may differ from the reference program's by a relative error of at most 0.001.
Values sent between devices are 32-bit elements; how exact they have to be, the bound alone decides.
A program may use at most 128 MiB of HBM per device.

```python
import math
import jax
import jax.numpy as jnp
import numpy as np
from jax import lax

DH = 128
HEADS = 24
TOKENS = 16384
DOCS = 8
DOC_MOST = 8192


def draw_queries(key, part):
    columns = jnp.arange(HEADS * DH) // DH
    rising = 10.0 ** (columns.astype(jnp.float32) / max(HEADS - 1, 1))
    base = jax.random.truncated_normal(key, -4.0, 4.0, (TOKENS, HEADS * DH), jnp.float32)
    return (0.25 * base * rising[None, :]).astype(jnp.bfloat16)


def block_levels(rng, shape, cuts, least, high):
    def one(axis_at, parts):
        steps = jax.random.uniform(jax.random.fold_in(jax.random.fold_in(rng, 6), axis_at), (parts,), jnp.float32, least / len(cuts), high / len(cuts))
        return jnp.repeat(jnp.exp(steps), shape[axis_at] // parts).reshape((-1,) + (1,) * (len(shape) - axis_at - 1))

    loudness = one(*cuts[0])
    for cut in cuts[1:]:
        loudness = loudness * one(*cut)
    return loudness


def length_profile(count, total, limit, lean):
    portions = [(1 << 20) // math.isqrt(standing ** lean) + 1 for standing in range(2, count + 1)]
    spare, holding = total - limit - (count - 1), [1] * (count - 1)
    while spare > 0:
        movable = [i for i in range(count - 1) if holding[i] < limit]
        pool, remaining = sum([portions[i] for i in movable]), spare
        for i in movable:
            extra = min(limit - holding[i], max(1, remaining * portions[i] // pool), spare)
            holding[i] = holding[i] + extra
            spare = spare - extra
    return np.array([limit] + holding)


def ragged_sizes(own_key, amount, total, most, skew):
    if amount == 2:
        one = jax.random.randint(own_key, (), max(1, total - most), min(most, total - 1) + 1)
        return jnp.stack([one, total - one])
    lengths = jnp.asarray(length_profile(amount, total, most, skew), jnp.int32)
    pairs = (amount - 1) // 2
    source_of, sink = lengths[1:1 + 2 * pairs:2], lengths[2:2 + 2 * pairs:2]
    slack = jnp.minimum(source_of - 1, most - sink)
    shifted = jax.random.randint(jax.random.fold_in(own_key, 1), (pairs,), 0, 1 << 20) % (slack + 1)
    lengths = lengths.at[1:1 + 2 * pairs:2].set(source_of - shifted).at[2:2 + 2 * pairs:2].set(sink + shifted)
    return lengths[jax.random.permutation(jax.random.fold_in(own_key, 2), amount)]


def centred(own_key, shape, width, reach, shards=(), dtype=jnp.bfloat16):
    factor_of = block_levels(own_key, shape, shards, -0.22, 0.18) if shards else 1.0
    result = jax.random.normal(own_key, shape, jnp.float32) * width * factor_of
    return jnp.minimum(jnp.maximum(result, -reach), reach).astype(dtype)


def setup_inputs(seed: int = 0) -> dict:
    key_of = jax.random.split(jax.random.key(seed), 6)
    return {
        "queries": draw_queries(jax.random.fold_in(key_of[5], 71), 0),
        "keys": centred(key_of[1], (TOKENS, HEADS * DH), 0.0883883476, 0.5, ((0, 8), (1, 4))),
        "values": centred(key_of[2], (TOKENS, HEADS * DH), 1.0, 6.0, ((0, 8), (1, 4))),
        "documents": jnp.searchsorted(jnp.cumsum(ragged_sizes(key_of[3], DOCS, TOKENS, DOC_MOST, 2)), jnp.arange(TOKENS), side="right").astype(jnp.int32),
        "norm_gain": jnp.clip(1.0 + 0.1 * jax.random.normal(key_of[4], (HEADS * DH,), jnp.float32), 0.5, 1.5),
    }


EPSILON = 1e-06

def reference(queries, keys, values, documents, norm_gain):
    block_rows = 64
    block_count = TOKENS // block_rows
    highest = lax.Precision.HIGHEST
    query_blocks = queries.reshape(block_count, block_rows, HEADS, DH)
    key_blocks = keys.reshape(block_count, block_rows, HEADS, DH)
    value_blocks = values.reshape(block_count, block_rows, HEADS, DH)
    doc_blocks = documents.reshape(block_count, block_rows)
    places = jnp.arange(block_rows)
    causal = places[:, None] >= places[None, :]
    gain_row = norm_gain.astype(jnp.float32)

    def advance(loop_carry, inputs):
        state_sum, doc_mark = loop_carry
        query_block, key_block, value_block, doc_block = inputs
        query_wide = query_block.astype(jnp.float32)
        key_wide = key_block.astype(jnp.float32)
        value_wide = value_block.astype(jnp.float32)
        scores = jnp.einsum('thd,shd->hts', query_wide, key_wide, precision=highest)
        keep_mask = causal & (doc_block[:, None] == doc_block[None, :])
        scores = jnp.where(keep_mask[None], scores, jnp.float32(0.0))
        within = jnp.einsum('hts,shd->thd', scores, value_wide, precision=highest)
        carried = jnp.einsum('thd,hde->the', query_wide, state_sum, precision=highest)
        live_rows = (doc_block + 1 == doc_mark)[:, None, None]
        mixed = within + jnp.where(live_rows, carried, jnp.float32(0.0))
        last_doc = doc_block[block_rows - 1]
        tail_rows = (doc_block == last_doc).astype(jnp.float32)
        block_state = jnp.einsum('thd,the->hde', key_wide * tail_rows[:, None, None], value_wide, precision=highest)
        state_sum = block_state + jnp.where(doc_mark == last_doc + 1, state_sum, jnp.float32(0.0))
        doc_mark = (last_doc + 1).astype(jnp.int32)
        flat_rows = mixed.reshape(block_rows, HEADS * DH)
        mean_square = lax.optimization_barrier(jnp.mean(flat_rows * flat_rows, axis=1, keepdims=True))
        normed = flat_rows * lax.rsqrt(mean_square + EPSILON) * gain_row
        return ((state_sum, doc_mark), normed.astype(jnp.bfloat16))
    start_carry = (jnp.zeros((HEADS, DH, DH), jnp.float32), jnp.zeros((), jnp.int32))
    _, outputs = lax.scan(advance, start_carry, (query_blocks, key_blocks, value_blocks, doc_blocks))
    return outputs.reshape(TOKENS, HEADS * DH)
```

```python
import functools

import jax
import jax.numpy as jnp
from jax import lax
from jax.experimental import pallas as pl
from jax.experimental.pallas import tpu as pltpu
from jax.sharding import PartitionSpec as P

DH = 128
BLOCK = 256
EXTRA = 8
DOC_MOST = 8192
EPSILON = 1e-06
F32 = jnp.float32
BF16 = jnp.bfloat16


def split(x):
    high = x.astype(BF16)
    return high, (x - high.astype(F32)).astype(BF16)


def dot(a, b):
    return lax.dot_general(a, b, (((1,), (0,)), ((), ())), preferred_element_type=F32)


def dot_nt(a, b):
    return lax.dot_general(a, b, (((1,), (1,)), ((), ())), preferred_element_type=F32)


def dot_tn(a, b):
    return lax.dot_general(a, b, (((0,), (0,)), ((), ())), preferred_element_type=F32)


def eye_mask():
    return lax.broadcasted_iota(jnp.int32, (BLOCK, BLOCK), 0) == lax.broadcasted_iota(
        jnp.int32, (BLOCK, BLOCK), 1
    )


def to_column(row):
    return jnp.sum(jnp.where(eye_mask(), row, 0.0), axis=1, keepdims=True)


def to_row(column):
    return jnp.sum(jnp.where(eye_mask(), column, 0.0), axis=0, keepdims=True)


def state_kernel(heads, blocks, k_ref, v_ref, d_ref, msg_ref):
    last = d_ref[blocks - 1 : blocks, BLOCK - 1 : BLOCK]
    totals = [None] * heads
    for b in range(blocks):
        tail = to_column(d_ref[b : b + 1, :]) == last
        rows = slice(b * BLOCK, (b + 1) * BLOCK)
        for h in range(heads):
            cols = slice(h * DH, (h + 1) * DH)
            key = jnp.where(tail, k_ref[rows, cols], jnp.zeros((), BF16))
            part = dot_tn(key, v_ref[rows, cols])
            totals[h] = part if totals[h] is None else totals[h] + part
    for h in range(heads):
        msg_ref[h, :DH, :] = totals[h]
        msg_ref[h, DH:, :] = jnp.broadcast_to(last, (EXTRA, DH))


def main_kernel(heads, q_ref, k_ref, v_ref, d_ref, o_ref, state, mark):
    b = pl.program_id(0)

    @pl.when(b == 0)
    def _():
        state[...] = jnp.zeros_like(state)
        mark[...] = jnp.zeros_like(mark)

    row = d_ref[0]
    column = to_column(row)
    causal = lax.broadcasted_iota(jnp.int32, (BLOCK, BLOCK), 0) >= lax.broadcasted_iota(
        jnp.int32, (BLOCK, BLOCK), 1
    )
    keep = causal & (column == row)
    before = mark[0:1, 0:1]
    live = column == before
    last = row[:, BLOCK - 1 : BLOCK]
    tail = column == last
    same = before == last
    for h in range(heads):
        cols = slice(h * DH, (h + 1) * DH)
        query, key, value = q_ref[:, cols], k_ref[:, cols], v_ref[:, cols]
        high, low = split(jnp.where(keep, dot_nt(query, key), 0.0))
        old = state[h]
        old_high, old_low = split(old)
        carried = dot(query, old_high) + dot(query, old_low)
        o_ref[:, cols] = dot(high, value) + dot(low, value) + jnp.where(live, carried, 0.0)
        fresh = dot_tn(jnp.where(tail, key, jnp.zeros((), BF16)), value)
        state[h] = fresh + jnp.where(same, old, 0.0)
    mark[...] = jnp.broadcast_to(last, mark.shape)


def correct_kernel(heads, a_ref, q_ref, d_ref, m_ref, o_ref, s_ref):
    column = to_column(d_ref[0])
    total = jnp.zeros((BLOCK, DH), F32)
    for h in range(heads):
        cols = slice(h * DH, (h + 1) * DH)
        high, low = split(m_ref[h, :DH, :])
        live = column == m_ref[h, DH : DH + 1, 0:1]
        query = q_ref[:, cols]
        whole = a_ref[:, cols] + jnp.where(live, dot(query, high) + dot(query, low), 0.0)
        o_ref[:, cols] = whole
        total = total + whole * whole
    s_ref[0] = to_row(jnp.sum(total, axis=1, keepdims=True))


def final_kernel(scale, a_ref, s_ref, g_ref, o_ref):
    factor = to_column(lax.rsqrt(s_ref[0] * scale + EPSILON))
    o_ref[...] = (a_ref[...] * factor * g_ref[...]).astype(BF16)


def join(newer, older):
    same = newer[:, DH : DH + 1, 0:1] == older[:, DH : DH + 1, 0:1]
    held = newer[:, :DH] + jnp.where(same, older[:, :DH], 0.0)
    return jnp.concatenate([held, newer[:, DH:]], axis=1)


def shards(queries, keys, values, documents, norm_gain):
    row_count, width = queries.shape
    heads = width // DH
    half = heads // 2
    blocks = row_count // BLOCK
    n = lax.axis_size("ctx")
    odd = lax.axis_index("ctx") % 2 == 1
    docs = (documents + 1).astype(F32).reshape(blocks, BLOCK)
    docs3 = docs.reshape(blocks, 1, BLOCK)
    params = pltpu.CompilerParams(vmem_limit_bytes=48 * 1024 * 1024)
    msg = pl.pallas_call(
        functools.partial(state_kernel, heads, blocks),
        out_shape=jax.ShapeDtypeStruct((heads, DH + EXTRA, DH), F32),
        compiler_params=params,
    )(keys, values, docs)
    swap = [(i, i ^ 1) for i in range(n)]
    ahead = [(i, i + 2) for i in range(n - 2)]
    own = jnp.where(odd, msg[half:], msg[:half])
    other = jnp.where(odd, msg[:half], msg[half:])
    got = lax.ppermute(other, "ctx", swap)
    first, second = jnp.where(odd, got, own), jnp.where(odd, own, got)
    steps = -(-(DOC_MOST - 1) // (2 * row_count))
    travel = join(second, first)
    reach = None
    for _ in range(steps):
        travel = lax.ppermute(travel, "ctx", ahead)
        reach = travel if reach is None else join(reach, travel)
    for_odd = join(first, reach)
    keep, give = jnp.where(odd, for_odd, reach), jnp.where(odd, reach, for_odd)
    got = lax.ppermute(give, "ctx", swap)
    incoming = jnp.concatenate([jnp.where(odd, got, keep), jnp.where(odd, keep, got)], axis=0)

    wide = pl.BlockSpec((BLOCK, width), lambda b: (b, 0))
    line = pl.BlockSpec((1, 1, BLOCK), lambda b: (b, 0, 0))
    local = pl.pallas_call(
        functools.partial(main_kernel, heads),
        grid=(blocks,),
        in_specs=[wide, wide, wide, line],
        out_specs=wide,
        out_shape=jax.ShapeDtypeStruct((row_count, width), F32),
        scratch_shapes=[pltpu.VMEM((heads, DH, DH), F32), pltpu.VMEM((8, DH), F32)],
        compiler_params=params,
        cost_estimate=pl.CostEstimate(
            flops=row_count * width * 2000, bytes_accessed=row_count * width * 10, transcendentals=0
        ),
    )(queries, keys, values, docs3)
    whole, squares = pl.pallas_call(
        functools.partial(correct_kernel, heads),
        grid=(blocks,),
        in_specs=[wide, wide, line, pl.BlockSpec((heads, DH + EXTRA, DH), lambda b: (0, 0, 0))],
        out_specs=[wide, line],
        out_shape=[
            jax.ShapeDtypeStruct((row_count, width), F32),
            jax.ShapeDtypeStruct((blocks, 1, BLOCK), F32),
        ],
        compiler_params=params,
    )(local, queries, docs3, incoming)
    total = lax.psum(squares, "head")
    scale = 1.0 / (width * lax.axis_size("head"))
    return pl.pallas_call(
        functools.partial(final_kernel, scale),
        grid=(blocks,),
        in_specs=[wide, line, pl.BlockSpec((1, width), lambda b: (0, 0))],
        out_specs=wide,
        out_shape=jax.ShapeDtypeStruct((row_count, width), BF16),
        compiler_params=params,
    )(whole, total, norm_gain[None, :])


def solution(mesh):
    return jax.shard_map(
        shards,
        mesh=mesh,
        in_specs=(P("ctx", "head"), P("ctx", "head"), P("ctx", "head"), P("ctx"), P("head")),
        out_specs=P("ctx", "head"),
        check_vma=False,
    )
```

```python
import functools

import jax
import jax.numpy as jnp
from jax import lax
from jax.experimental import pallas as pl
from jax.experimental.pallas import tpu as pltpu
from jax.sharding import PartitionSpec as P

DH = 128
BLOCK = 256
EXTRA = 8
DOC_MOST = 8192
EPSILON = 1e-06
F32 = jnp.float32
BF16 = jnp.bfloat16


def split(x):
    high = x.astype(BF16)
    return high, (x - high.astype(F32)).astype(BF16)


def dot(a, b):
    return lax.dot_general(a, b, (((1,), (0,)), ((), ())), preferred_element_type=F32)


def dot_nt(a, b):
    return lax.dot_general(a, b, (((1,), (1,)), ((), ())), preferred_element_type=F32)


def dot_tn(a, b):
    return lax.dot_general(a, b, (((0,), (0,)), ((), ())), preferred_element_type=F32)


def eye_mask():
    return lax.broadcasted_iota(jnp.int32, (BLOCK, BLOCK), 0) == lax.broadcasted_iota(
        jnp.int32, (BLOCK, BLOCK), 1
    )


def to_column(row):
    return jnp.sum(jnp.where(eye_mask(), row, 0.0), axis=1, keepdims=True)


def to_row(column):
    return jnp.sum(jnp.where(eye_mask(), column, 0.0), axis=0, keepdims=True)


def join(newer, older):
    same = newer[DH : DH + 1, 0:1] == older[DH : DH + 1, 0:1]
    return newer[:DH] + jnp.where(same, older[:DH], 0.0), newer[DH:]


def carry_in(query, pair):
    both = dot(query, pair)
    return both[:, :DH] + both[:, DH:]


def fused_kernel(heads, blocks, steps, n, nh, scale, *refs):
    (q_ref, k_ref, v_ref, d_ref, g_ref, o_ref, whole, state, mark, sent, got, travel, give, back,
     incoming, pairs, squares, others, send_a, recv_a, send_t, recv_t, send_b, recv_b, send_s,
     recv_s) = refs
    half = heads // 2
    me, place = lax.axis_index("ctx"), lax.axis_index("head")
    odd = lax.rem(me, 2)
    is_odd = odd == 1
    partner = me + 1 - 2 * odd
    ahead = lax.rem(me + 2, n)
    behind = lax.rem(me + n - 2, n)
    has_next, has_prev = me < n - 2, me >= 2
    own, other = odd * half, (1 - odd) * half

    def copy(source, target, send, recv, ctx, head):
        return pltpu.make_async_remote_copy(
            src_ref=source,
            dst_ref=target,
            send_sem=send,
            recv_sem=recv,
            device_id=(ctx, head),
            device_id_type=pl.DeviceIdType.MESH,
        )

    barrier = pltpu.get_barrier_semaphore()

    def greet(ctx, head):
        pl.semaphore_signal(
            barrier, inc=1, device_id=(ctx, head), device_id_type=pl.DeviceIdType.MESH
        )

    greet(partner, place)
    for j in range(1, nh):
        greet(me, lax.rem(place + j, nh))

    greet(ahead, place)
    greet(behind, place)

    last = d_ref[blocks - 1][:, BLOCK - 1 : BLOCK]
    tails = [to_column(d_ref[b]) == last for b in range(blocks)]

    def local_state(h):
        cols = pl.ds(pl.multiple_of(h * DH, DH), DH)
        total = None
        for b in range(blocks):
            rows = slice(b * BLOCK, (b + 1) * BLOCK)
            key = jnp.where(tails[b], k_ref[rows, cols], jnp.zeros((), BF16))
            part = dot_tn(key, v_ref[rows, cols])
            total = part if total is None else total + part
        sent[h, :DH, :] = total
        sent[h, DH:, :] = jnp.broadcast_to(last, (EXTRA, DH))

    swap_a = [
        copy(sent.at[other + i], got.at[i], send_a.at[i], recv_a.at[i], partner, place)
        for i in range(half)
    ]
    hops = [
        [
            copy(
                travel.at[t, i], travel.at[t + 1, i], send_t.at[t, i], recv_t.at[t, i], ahead, place
            )
            for i in range(half)
        ]
        for t in range(steps)
    ]
    swap_b = [
        copy(give.at[i], back.at[i], send_b.at[i], recv_b.at[i], partner, place)
        for i in range(half)
    ]
    for i in range(half):
        local_state(other + i)
        if i == 0:
            pl.semaphore_wait(barrier, nh + 2)
        swap_a[i].start()
    for i in range(half):
        local_state(own + i)

    @pl.when(me < 2)
    def _():
        for t in range(steps):
            travel[t + 1] = jnp.zeros((half, DH + EXTRA, DH), F32)

    state[...] = jnp.zeros_like(state)
    mark[...] = jnp.zeros_like(mark)
    causal = lax.broadcasted_iota(jnp.int32, (BLOCK, BLOCK), 0) >= lax.broadcasted_iota(
        jnp.int32, (BLOCK, BLOCK), 1
    )

    def block_step(b, carry):
        rows = pl.ds(pl.multiple_of(b * BLOCK, BLOCK), BLOCK)
        row = d_ref[b]
        column = to_column(row)
        keep = causal & (column == row)
        before = mark[0:1, 0:1]
        live = column == before
        final = row[:, BLOCK - 1 : BLOCK]
        tail = column == final
        same = before == final
        for h in range(heads):
            cols = slice(h * DH, (h + 1) * DH)
            query, key, value = q_ref[rows, cols], k_ref[rows, cols], v_ref[rows, cols]
            high, low = split(jnp.where(keep, dot_nt(query, key), 0.0))
            old = state[h]
            carried = carry_in(query, jnp.concatenate(split(old), axis=1))
            whole[rows, cols] = dot(high, value) + dot(low, value) + jnp.where(live, carried, 0.0)
            fresh = dot_tn(jnp.where(tail, key, jnp.zeros((), BF16)), value)
            state[h] = fresh + jnp.where(same, old, 0.0)
        mark[...] = jnp.broadcast_to(final, mark.shape)
        return carry

    def first_of(i):
        return jnp.where(is_odd, got[i], sent[own + i])

    cuts = [(blocks * j) // (steps + 2) for j in range(steps + 3)]
    lax.fori_loop(cuts[0], cuts[1], block_step, 0)
    for i in range(half):
        swap_a[i].wait_recv()
        held, tag = join(jnp.where(is_odd, sent[own + i], got[i]), first_of(i))
        travel[0, i, :DH, :] = held
        travel[0, i, DH:, :] = tag

        @pl.when(has_next)
        def _():
            hops[0][i].start()

    for t in range(1, steps):
        lax.fori_loop(cuts[t], cuts[t + 1], block_step, 0)
        for i in range(half):

            @pl.when(has_prev)
            def _():
                hops[t - 1][i].wait_recv()

            @pl.when(has_next)
            def _():
                hops[t][i].start()

    lax.fori_loop(cuts[steps], cuts[steps + 1], block_step, 0)
    for i in range(half):

        @pl.when(has_prev)
        def _():
            hops[steps - 1][i].wait_recv()

        reach = travel[1, i]
        for t in range(1, steps):
            reach = jnp.concatenate(join(reach, travel[t + 1, i]), axis=0)
        for_odd = jnp.concatenate(join(first_of(i), reach), axis=0)
        give[i] = jnp.where(is_odd, reach, for_odd)
        swap_b[i].start()
        incoming[own + i] = jnp.where(is_odd, for_odd, reach)
    lax.fori_loop(cuts[steps + 1], cuts[steps + 2], block_step, 0)
    for i in range(half):
        swap_b[i].wait_recv()
        incoming[other + i] = back[i]
    for h in range(heads):
        pairs[h] = jnp.concatenate(split(incoming[h, :DH, :]), axis=1)
    target = incoming[0, DH : DH + 1, 0:1]

    def correct_step(b, carry):
        rows = pl.ds(pl.multiple_of(b * BLOCK, BLOCK), BLOCK)
        live = to_column(d_ref[b]) == target
        total = jnp.zeros((BLOCK, DH), F32)
        for h in range(heads):
            cols = slice(h * DH, (h + 1) * DH)
            fixed = whole[rows, cols] + jnp.where(live, carry_in(q_ref[rows, cols], pairs[h]), 0.0)
            whole[rows, cols] = fixed
            total = total + fixed * fixed
        squares[b] = to_row(jnp.sum(total, axis=1, keepdims=True))
        return carry

    lax.fori_loop(0, blocks, correct_step, 0)
    sums = [
        copy(
            squares,
            others.at[j - 1],
            send_s.at[j - 1],
            recv_s.at[j - 1],
            me,
            lax.rem(place + j, nh),
        )
        for j in range(1, nh)
    ]
    for item in sums:
        item.start()
    for item in sums:
        item.wait_recv()

    def final_step(b, carry):
        rows = pl.ds(pl.multiple_of(b * BLOCK, BLOCK), BLOCK)
        total = squares[b]
        for j in range(nh - 1):
            total = total + others[j, b]
        factor = to_column(lax.rsqrt(total * scale + EPSILON))
        for h in range(heads):
            cols = slice(h * DH, (h + 1) * DH)
            o_ref[rows, cols] = (whole[rows, cols] * factor * g_ref[:, cols]).astype(BF16)
        return carry

    lax.fori_loop(0, blocks, final_step, 0)
    for item in swap_a + swap_b + sums:
        item.wait_send()

    @pl.when(has_next)
    def _():
        for hop in hops:
            for item in hop:
                item.wait_send()


def shards(queries, keys, values, documents, norm_gain):
    row_count, width = queries.shape
    heads = width // DH
    half = heads // 2
    blocks = row_count // BLOCK
    n, nh = lax.axis_size("ctx"), lax.axis_size("head")
    steps = -(-(DOC_MOST - 1) // (2 * row_count))
    docs = (documents + 1).astype(F32).reshape(blocks, 1, BLOCK)
    message = (DH + EXTRA, DH)
    dma = pltpu.SemaphoreType.DMA
    vmem = pl.BlockSpec(memory_space=pltpu.VMEM)
    return pl.pallas_call(
        functools.partial(fused_kernel, heads, blocks, steps, n, nh, 1.0 / (width * nh)),
        in_specs=[vmem] * 5,
        out_specs=vmem,
        out_shape=jax.ShapeDtypeStruct((row_count, width), BF16),
        scratch_shapes=[
            pltpu.VMEM((row_count, width), F32),
            pltpu.VMEM((heads, DH, DH), F32),
            pltpu.VMEM((8, DH), F32),
            pltpu.VMEM((heads, *message), F32),
            pltpu.VMEM((half, *message), F32),
            pltpu.VMEM((steps + 1, half, *message), F32),
            pltpu.VMEM((half, *message), F32),
            pltpu.VMEM((half, *message), F32),
            pltpu.VMEM((heads, *message), F32),
            pltpu.VMEM((heads, DH, 2 * DH), BF16),
            pltpu.VMEM((blocks, 1, BLOCK), F32),
            pltpu.VMEM((nh - 1, blocks, 1, BLOCK), F32),
            dma((half,)),
            dma((half,)),
            dma((steps, half)),
            dma((steps, half)),
            dma((half,)),
            dma((half,)),
            dma((nh - 1,)),
            dma((nh - 1,)),
        ],
        compiler_params=pltpu.CompilerParams(
            vmem_limit_bytes=56 * 1024 * 1024, collective_id=0, has_side_effects=True
        ),
    )(queries, keys, values, docs, norm_gain[None, :])


def solution(mesh):
    return jax.shard_map(
        shards,
        mesh=mesh,
        in_specs=(P("ctx", "head"), P("ctx", "head"), P("ctx", "head"), P("ctx"), P("head")),
        out_specs=P("ctx", "head"),
        check_vma=False,
    )
```
